32 devices in a mesh: cand: 16 (over z, x, core), query: 2 (over y).
Axes of the slice: x: 2, y: 2, z: 4, core: 2. Of those that a mesh axis runs over, the one named last changes fastest.
Arguments:
- pool: bfloat16 [40960, 4096], P(('cand', 'query')), may hold values from -6 to 6
- cand_ids: int32 [32768], P(('cand', 'query')), may hold values from 0 to 1279
- pick_ids: int32 [32], P(('cand', 'query')), may hold values from 0 to 1279
- queries: bfloat16 [256, 4096], P('query'), may hold values from -6 to 6
Outputs:
- gains: float32 [32768], P(('cand', 'query'))
- coverage: float32 [256], P('query')
The draws below stay inside these ranges and needn't reach their ends.
Inputs may be any that keep to these rules, and one draw needn't show every extreme that they name: `cand_ids`: each id is a row within the pool block of 1280 rows that lies on the same device as the id. `pick_ids`: each id is a row within the pool block of 1280 rows that lies on the same device as the id.
All inputs are finite; a program needn't handle non-finite values.
Results may differ from the reference program's by a relative error of at most 0.0003.
Values may be sent and summed in bfloat16 or wider, within the bound.
No kernel may reach another device: no remote copies, remote signals or barrier semaphores. Data moves between devices by JAX's collectives and lax.ppermute only.
A program may use at most 128 MiB of HBM per device.

```python
import math
import jax
import jax.numpy as jnp
from jax import lax

D = 4096
CAND_DEV = 1024
PICK_DEV = 1
POOL_DEV = 1280
CANDS = 32768
PICKS = 32
POOL = 40960
Q = 256


def set_ends(values, key, least, largest):
    shape = values.shape
    spot = [jax.random.randint(jax.random.fold_in(key, axis), (), 0, shape[axis]) for axis in range(len(shape))]
    values = values.at[tuple(spot)].set(least)
    longest = shape.index(max(shape))
    spot[longest] = (spot[longest] + 1) % shape[longest]
    return values.at[tuple(spot)].set(largest)


def level_of(rng, dims, shards, low, largest):
    level = 1.0
    for dim, shards_of in shards:
        draws = jax.random.uniform(jax.random.fold_in(jax.random.fold_in(rng, 6), dim), (shards_of,), jnp.float32, low / len(shards), largest / len(shards))
        level = level * jnp.repeat(jnp.exp(draws), dims[dim] // shards_of).reshape((-1,) + (1,) * (len(dims) - 1 - dim))
    return level


def scatter_about(key, dims, spread, limit, shards=(), kind=jnp.bfloat16):
    drawn = spread * jax.random.normal(key, dims, jnp.float32)
    if shards:
        drawn = drawn * level_of(key, dims, shards, -0.22, 0.18)
    return jnp.clip(drawn, -limit, limit).astype(kind)


def setup_inputs(seed: int = 0) -> dict:
    keys = jax.random.split(jax.random.key(seed), 5)
    pool = scatter_about(keys[0], (POOL, D), 1.0, 6.0, ((0, 32),))
    cand_ids = set_ends(jax.random.randint(keys[1], (CANDS,), 0, POOL_DEV), jax.random.fold_in(keys[1], 1), 0, POOL_DEV - 1).astype(jnp.int32)
    pick_ids = set_ends(jax.random.randint(keys[2], (PICKS,), 0, POOL_DEV), jax.random.fold_in(keys[2], 1), 0, POOL_DEV - 1).astype(jnp.int32)
    queries = scatter_about(keys[3], (Q, D), 1.0, 6.0, ((0, 2),))
    return dict(pool=pool, cand_ids=cand_ids, pick_ids=pick_ids, queries=queries)


def similarity(rows, targets):
    product = lax.dot_general(rows, targets, (((1,), (1,)), ((), ())), preferred_element_type=jnp.float32)
    return product * (1.0 / math.sqrt(D))

def reference(pool, cand_ids, pick_ids, queries):
    blocks = pool.shape[0] // POOL_DEV
    pool_blocks = pool.reshape(blocks, POOL_DEV, D)
    cand_blocks = cand_ids.reshape(blocks, CAND_DEV)
    pick_blocks = pick_ids.reshape(blocks, PICK_DEV)

    def pick_best(args):
        rows, ids = args
        return lax.optimization_barrier(jnp.max(similarity(rows[ids], queries), axis=0))
    coverage = lax.optimization_barrier(jnp.max(lax.map(pick_best, (pool_blocks, pick_blocks)), axis=0))

    def cand_gain(args):
        rows, ids = args
        scores = similarity(rows[ids], queries)
        gained = lax.optimization_barrier(jnp.sum(jnp.maximum(scores - coverage[None, :], 0.0), axis=1))
        return gained + 1.0 * lax.optimization_barrier(jnp.max(scores, axis=1))
    gains = lax.map(cand_gain, (pool_blocks, cand_blocks)).reshape(-1)
    return (gains, coverage)
```

```python
import functools
import math

import jax
import jax.numpy as jnp
from jax import lax
from jax.experimental import pallas as pl
from jax.experimental.pallas import tpu as pltpu
from jax.sharding import PartitionSpec as P

LANES = 128
CHUNKS = 2
NT = (((1,), (1,)), ((), ()))
VMEM = pl.BlockSpec(memory_space=pltpu.VMEM)
PARAMS = pltpu.CompilerParams(vmem_limit_bytes=12 * 2**20)


def dot(rows, targets):
    return lax.dot_general(rows, targets, NT, preferred_element_type=jnp.float32)


def block_of(rows):
    return math.gcd(rows, 2 * LANES)


def scores_kernel(start, width, pool, *refs):
    *targets, out = refs
    step = block_of(pool.shape[0])
    targets = jnp.concatenate([t[...] for t in targets], axis=0)
    for row in range(0, pool.shape[0], step):
        out[row : row + step, :] = dot(
            pool[row : row + step, start : start + width], targets
        )


def scores(pool, targets, start):
    rows, width = pool.shape[0], targets[0].shape[1]
    count = sum(t.shape[0] for t in targets)
    return pl.pallas_call(
        functools.partial(scores_kernel, start, width),
        in_specs=[VMEM] * (1 + len(targets)),
        out_specs=VMEM,
        out_shape=jax.ShapeDtypeStruct((rows, count), jnp.float32),
        compiler_params=PARAMS,
        cost_estimate=pl.CostEstimate(
            flops=2 * rows * max(count, 256) * width,
            bytes_accessed=rows * width * 2,
            transcendentals=0,
        ),
        name="scores",
    )(pool, *targets)


def gains_kernel(scale, groups, picks, ids, *refs):
    gains, cover, wide = refs[-3:]
    refs = list(refs[:-3])
    parts, pieces = [], []
    for n_parts, n_pieces in groups:
        parts.append([refs.pop(0) for _ in range(n_parts)])
        pieces.append([[refs.pop(0) for _ in range(n_pieces)] for _ in range(n_parts)])
    n_picks, cut, _ = picks.shape
    lines = math.gcd(cut, 4)
    width = lines * LANES

    wide[...] = picks[...].astype(jnp.float32).reshape(n_picks * cut, LANES)
    covers = []
    total = None
    for j in range(cut // lines):
        rows = jnp.concatenate(
            [
                wide[pl.ds(j * lines + k, n_picks, stride=cut), :]
                for k in range(lines)
            ],
            axis=1,
        ).astype(jnp.bfloat16)
        blocks = []
        for part in pieces:
            held = part[0][0].shape[1]
            part_of = part[(j * width) // held]
            at = (j * width) % held
            blocks += [piece[:, at : at + width] for piece in part_of]
        term = dot(rows, jnp.concatenate(blocks, axis=0))
        total = term if total is None else total + term
    best = jnp.max(total, axis=0, keepdims=True)
    at = 0
    for part in parts:
        count = part[0].shape[1]
        covers.append(best[:, at : at + count])
        at += count
    cover[...] = covers[0] * scale

    row = lax.broadcasted_iota(jnp.int32, (LANES, LANES), 0)
    lane = lax.broadcasted_iota(jnp.int32, (LANES, LANES), 1)
    diagonal = row == lane
    wanted = ids[...]
    block_wanted, lane_wanted = wanted // LANES, wanted % LANES
    found = jnp.zeros(wanted.shape, jnp.float32)
    for block in range(parts[0][0].shape[0] // LANES):
        above, highest = None, None
        for part, covered in zip(parts, covers):
            s = part[0][block * LANES : (block + 1) * LANES, :]
            for other in part[1:]:
                s = s + other[block * LANES : (block + 1) * LANES, :]
            over = jnp.maximum(s - covered, 0.0)
            above = over if above is None else above + over
            highest = s if highest is None else jnp.maximum(highest, s)
        gain = jnp.sum(above, axis=1, keepdims=True) + 1.0 * jnp.max(
            highest, axis=1, keepdims=True
        )
        line = jnp.sum(jnp.where(diagonal, gain, 0.0), axis=0, keepdims=True)
        table = jnp.broadcast_to(line, wanted.shape)
        here = jnp.take_along_axis(table, lane_wanted, axis=1, mode="promise_in_bounds")
        found = jnp.where(block_wanted == block, here, found)
    gains[...] = found * scale


def gains_of(picks, ids, blocks, scale):
    groups = tuple((len(parts), len(pieces[0])) for parts, pieces in blocks)
    flat = []
    for parts, pieces in blocks:
        flat += list(parts)
        for some in pieces:
            flat += list(some)
    count = blocks[0][0][0].shape[1]
    n_picks, cut, _ = picks.shape
    return pl.pallas_call(
        functools.partial(gains_kernel, scale, groups),
        in_specs=[VMEM] * (2 + len(flat)),
        out_shape=(
            jax.ShapeDtypeStruct(ids.shape, jnp.float32),
            jax.ShapeDtypeStruct((1, count), jnp.float32),
        ),
        scratch_shapes=[pltpu.VMEM((n_picks * cut, LANES), jnp.float32)],
        compiler_params=PARAMS,
        name="gains",
    )(picks, ids, *flat)


def gather_over(x, axis, size):
    if size & (size - 1):
        rest = [
            lax.ppermute(x, axis, [(i, (i + s) % size) for i in range(size)])
            for s in range(1, size)
        ]
        return jnp.concatenate([x] + rest, axis=0)
    bit = size // 2
    while bit:
        got = lax.ppermute(x, axis, [(i, i ^ bit) for i in range(size)])
        x = jnp.concatenate([x, got], axis=0)
        bit //= 2
    return x


def on_device(sizes, pool, cand_ids, pick_ids, queries):
    n_cand, n_query = sizes
    depth = pool.shape[1]
    scale = 1.0 / math.sqrt(depth)

    picks = jnp.concatenate(
        [
            lax.dynamic_slice_in_dim(pool, pick_ids[i], 1, 0)
            for i in range(pick_ids.shape[0])
        ],
        axis=0,
    ).reshape(pick_ids.shape[0], depth // LANES, LANES)
    picks = gather_over(picks, "query", n_query)
    picks = gather_over(picks, "cand", n_cand)

    share = 2 if n_cand % 2 == 0 else 1
    count = queries.shape[0] // share
    width = depth // CHUNKS
    mine = lax.rem(lax.axis_index("cand"), share) * count
    blocks = [([scores(pool, [queries], 0)], [[queries]])]
    for shift in range(1, n_query):
        parts, pieces = [], []
        for chunk in range(CHUNKS):
            piece = lax.dynamic_slice(queries, (mine, chunk * width), (count, width))
            got = lax.ppermute(
                piece, "query", [(i, (i + shift) % n_query) for i in range(n_query)]
            )
            held = [got]
            if share == 2:
                held.append(
                    lax.ppermute(got, "cand", [(i, i ^ 1) for i in range(n_cand)])
                )
            parts.append(scores(pool, held, chunk * width))
            pieces.append(held)
        blocks.append((parts, pieces))

    ids = cand_ids.reshape(-1, LANES)
    gains, cover = gains_of(picks, ids, blocks, scale)
    return gains.reshape(cand_ids.shape), cover.reshape(queries.shape[:1])


def solution(mesh):
    sizes = (mesh.shape["cand"], mesh.shape["query"])
    in_specs = (
        P(("cand", "query"), None),
        P(("cand", "query")),
        P(("cand", "query")),
        P("query", None),
    )
    out_specs = (P(("cand", "query")), P("query"))
    return jax.shard_map(
        functools.partial(on_device, sizes),
        mesh=mesh,
        in_specs=in_specs,
        out_specs=out_specs,
        check_vma=False,
    )
```

```python
import functools
import math

import jax
import jax.numpy as jnp
from jax import lax
from jax.experimental import pallas as pl
from jax.experimental.pallas import tpu as pltpu
from jax.sharding import PartitionSpec as P

LANES = 128
SUBLANES = 8
CHUNKS = 2
OWN = 2
NT = (((1,), (1,)), ((), ()))
VMEM = pl.BlockSpec(memory_space=pltpu.VMEM)
SMEM = pl.BlockSpec(memory_space=pltpu.SMEM)
HBM = pl.BlockSpec(memory_space=pltpu.HBM)
PARAMS = pltpu.CompilerParams(vmem_limit_bytes=12 * 2**20)


def dot(rows, targets):
    return lax.dot_general(rows, targets, NT, preferred_element_type=jnp.float32)


def block_of(rows):
    return math.gcd(rows, 2 * LANES)


def cost(rows, count, width, read=0):
    return pl.CostEstimate(
        flops=2 * rows * max(count, 256) * width,
        bytes_accessed=rows * width * 2 + read,
        transcendentals=0,
    )


def start_kernel(share, pick_ids, pool, queries, *refs):
    picks, held, *pieces, tile, lines, pick_sem, sems = refs
    n_picks, cut, _ = picks.shape
    count, width = pieces[0].shape
    mine = pl.multiple_of(lax.rem(lax.axis_index("cand"), share) * count, count)
    moves = []
    for k, piece in enumerate(pieces):
        source = queries.at[pl.ds(mine, count), k * width : (k + 1) * width]
        moves.append(pltpu.make_async_copy(source, piece, sems.at[k]))
    moves.append(pltpu.make_async_copy(queries, held, sems.at[len(pieces)]))
    copies = []
    for i in range(n_picks):
        at = pl.multiple_of(pick_ids[i] // SUBLANES * SUBLANES, SUBLANES)
        copies.append(
            pltpu.make_async_copy(
                pool.at[pl.ds(at, SUBLANES), :], tile.at[i], pick_sem.at[i]
            )
        )
        copies[-1].start()
    for move in moves:
        move.start()
    row = lax.broadcasted_iota(jnp.int32, (SUBLANES, LANES), 0)
    for i in range(n_picks):
        copies[i].wait()
        own = row == pick_ids[i] % SUBLANES
        for c in range(cut):
            some = tile[i, :, c * LANES : (c + 1) * LANES].astype(jnp.float32)
            lines[c : c + 1, :] = jnp.sum(
                jnp.where(own, some, 0.0), axis=0, keepdims=True
            )
        picks[i] = lines[...].astype(jnp.bfloat16)
    for move in moves:
        move.wait()


def start(pool, pick_ids, queries, share):
    n_picks, depth = pick_ids.shape[0], pool.shape[1]
    piece = jax.ShapeDtypeStruct(
        (queries.shape[0] // share, depth // CHUNKS), queries.dtype
    )
    return pl.pallas_call(
        functools.partial(start_kernel, share),
        in_specs=[SMEM, HBM, HBM],
        out_specs=[VMEM] * (2 + CHUNKS),
        out_shape=[
            jax.ShapeDtypeStruct((n_picks, depth // LANES, LANES), pool.dtype),
            jax.ShapeDtypeStruct(queries.shape, queries.dtype),
        ]
        + [piece] * CHUNKS,
        scratch_shapes=[
            pltpu.VMEM((n_picks, SUBLANES, depth), pool.dtype),
            pltpu.VMEM((depth // LANES, LANES), jnp.float32),
            pltpu.SemaphoreType.DMA((n_picks,)),
            pltpu.SemaphoreType.DMA((CHUNKS + 1,)),
        ],
        compiler_params=PARAMS,
        cost_estimate=cost(0, 0, 0, 8 * pool.size),
        name="start",
    )(
        pick_ids,
        pltpu.with_memory_space_constraint(pool, pltpu.HBM),
        pltpu.with_memory_space_constraint(queries, pltpu.HBM),
    )


def scores_kernel(first, start, width, pool, *refs):
    targets, out = refs[:-1], refs[-1]
    targets = jnp.concatenate([t[...] for t in targets], axis=0)
    step = block_of(out.shape[0])
    for row in range(0, out.shape[0], step):
        out[row : row + step, :] = dot(
            pool[first + row : first + row + step, start : start + width], targets
        )


def scores(pool, targets, start, first, rows):
    width = targets[0].shape[1]
    count = sum(t.shape[0] for t in targets)
    return pl.pallas_call(
        functools.partial(scores_kernel, first, start, width),
        in_specs=[VMEM] * (1 + len(targets)),
        out_specs=VMEM,
        out_shape=jax.ShapeDtypeStruct((rows, count), jnp.float32),
        compiler_params=PARAMS,
        cost_estimate=cost(rows, count, width),
        name="scores",
    )(pool, *targets)


def gains_kernel(scale, sizes, groups, picks, ids, *refs):
    gains, cover, wide = refs[-3:]
    refs = list(refs[:-3])
    own = [refs.pop(0) for _ in sizes]
    parts, pieces = [], [[[refs.pop(0)]]]
    for n_parts, n_pieces in groups:
        parts.append([refs.pop(0) for _ in range(n_parts)])
        pieces.append([[refs.pop(0) for _ in range(n_pieces)] for _ in range(n_parts)])
    n_picks, cut, _ = picks.shape
    lines = math.gcd(cut, 4)
    width = lines * LANES

    wide[...] = picks[...].astype(jnp.float32).reshape(n_picks * cut, LANES)
    total = None
    for j in range(cut // lines):
        rows = jnp.concatenate(
            [
                wide[pl.ds(j * lines + k, n_picks, stride=cut), :]
                for k in range(lines)
            ],
            axis=1,
        ).astype(jnp.bfloat16)
        blocks = []
        for part in pieces:
            held = part[0][0].shape[1]
            part_of = part[(j * width) // held]
            at = (j * width) % held
            blocks += [piece[:, at : at + width] for piece in part_of]
        term = dot(rows, jnp.concatenate(blocks, axis=0))
        total = term if total is None else total + term
    best = jnp.max(total, axis=0, keepdims=True)
    covers, at = [], 0
    for count in [own[0].shape[1]] + [part[0].shape[1] for part in parts]:
        covers.append(best[:, at : at + count])
        at += count
    cover[...] = covers[0] * scale

    row = lax.broadcasted_iota(jnp.int32, (LANES, LANES), 0)
    lane = lax.broadcasted_iota(jnp.int32, (LANES, LANES), 1)
    diagonal = row == lane
    wanted = ids[...]
    block_wanted, lane_wanted = wanted // LANES, wanted % LANES
    found = jnp.zeros(wanted.shape, jnp.float32)
    block = 0
    for rows_of, size in zip(own, sizes):
        for k in range(size // LANES):
            some = slice(block * LANES, (block + 1) * LANES)
            every = [rows_of[k * LANES : (k + 1) * LANES, :]]
            for part in parts:
                s = part[0][some, :]
                for other in part[1:]:
                    s = s + other[some, :]
                every.append(s)
            above, highest = None, None
            for s, covered in zip(every, covers):
                over = jnp.maximum(s - covered, 0.0)
                above = over if above is None else above + over
                highest = s if highest is None else jnp.maximum(highest, s)
            gain = jnp.sum(above, axis=1, keepdims=True) + 1.0 * jnp.max(
                highest, axis=1, keepdims=True
            )
            line = jnp.sum(jnp.where(diagonal, gain, 0.0), axis=0, keepdims=True)
            table = jnp.broadcast_to(line, wanted.shape)
            here = jnp.take_along_axis(
                table, lane_wanted, axis=1, mode="promise_in_bounds"
            )
            found = jnp.where(block_wanted == block, here, found)
            block += 1
    gains[...] = found * scale


def gains_of(picks, ids, own, queries, blocks, scale):
    sizes = tuple(o.shape[0] for o in own)
    groups = tuple((len(parts), len(pieces[0])) for parts, pieces in blocks)
    flat = list(own) + [queries]
    for parts, pieces in blocks:
        flat += list(parts)
        for some in pieces:
            flat += list(some)
    n_picks, cut, _ = picks.shape
    return pl.pallas_call(
        functools.partial(gains_kernel, scale, sizes, groups),
        in_specs=[VMEM] * (2 + len(flat)),
        out_shape=(
            jax.ShapeDtypeStruct(ids.shape, jnp.float32),
            jax.ShapeDtypeStruct((1, queries.shape[0]), jnp.float32),
        ),
        scratch_shapes=[pltpu.VMEM((n_picks * cut, LANES), jnp.float32)],
        compiler_params=PARAMS,
        name="gains",
    )(picks, ids, *flat)


def strides(size):
    if size & (size - 1):
        return None
    return [size >> (k + 1) for k in range(size.bit_length() - 1)]


def gather_over(x, axis, size):
    if strides(size) is None:
        rest = [
            lax.ppermute(x, axis, [(i, (i + s) % size) for i in range(size)])
            for s in range(1, size)
        ]
        return jnp.concatenate([x] + rest, axis=0)
    for bit in strides(size):
        got = lax.ppermute(x, axis, [(i, i ^ bit) for i in range(size)])
        x = jnp.concatenate([x, got], axis=0)
    return x


def on_device(sizes, pool, cand_ids, pick_ids, queries):
    n_cand, n_query = sizes
    rows, depth = pool.shape
    scale = 1.0 / math.sqrt(depth)

    share = 2 if n_cand % 2 == 0 else 1
    width = depth // CHUNKS
    picks, held, *sent = start(pool, pick_ids, queries, share)
    picks = gather_over(picks, "query", n_query)
    picks = gather_over(picks, "cand", n_cand)

    own, first = [], 0
    for k in range(OWN):
        some = rows * (k + 1) // OWN // LANES * LANES - first
        own.append(scores(pool, [held], 0, first, some))
        first += some

    blocks = []
    for shift in range(1, n_query):
        parts, pieces = [], []
        for chunk in range(CHUNKS):
            got = lax.ppermute(
                sent[chunk],
                "query",
                [(i, (i + shift) % n_query) for i in range(n_query)],
            )
            both = [got]
            if share == 2:
                both.append(
                    lax.ppermute(got, "cand", [(i, i ^ 1) for i in range(n_cand)])
                )
            parts.append(scores(pool, both, chunk * width, 0, rows))
            pieces.append(both)
        blocks.append((parts, pieces))

    ids = cand_ids.reshape(-1, LANES)
    gains, cover = gains_of(picks, ids, own, held, blocks, scale)
    return gains.reshape(cand_ids.shape), cover.reshape(queries.shape[:1])


def solution(mesh):
    sizes = (mesh.shape["cand"], mesh.shape["query"])
    in_specs = (
        P(("cand", "query"), None),
        P(("cand", "query")),
        P(("cand", "query")),
        P("query", None),
    )
    out_specs = (P(("cand", "query")), P("query"))

    def body(*args):
        return on_device(sizes, *args)

    return jax.shard_map(
        body, mesh=mesh, in_specs=in_specs, out_specs=out_specs, check_vma=False
    )
```

```python
import functools
import math

import jax
import jax.numpy as jnp
from jax import lax
from jax.experimental import pallas as pl
from jax.experimental.pallas import tpu as pltpu
from jax.sharding import PartitionSpec as P

LANES = 128
SUBLANES = 8
PARTS = (2, 1)
ROWS = 640
NT = (((1,), (1,)), ((), ()))
VMEM = pl.BlockSpec(memory_space=pltpu.VMEM)
HBM = pl.BlockSpec(memory_space=pltpu.HBM)
PARAMS = pltpu.CompilerParams(vmem_limit_bytes=12 * 2**20)


def dot(rows, targets):
    return lax.dot_general(rows, targets, NT, preferred_element_type=jnp.float32)


def cost(rows, count, width, read=0):
    return pl.CostEstimate(
        flops=2 * rows * max(count, 256) * width,
        bytes_accessed=rows * width * 2 + read,
        transcendentals=0,
    )


def start_kernel(share, pick_ids, pool, queries, *refs):
    picks, *pieces, tile, lines, pick_sem, sems = refs
    n_picks, cut, _ = picks.shape
    count = pieces[0].shape[0]
    wanted = [jnp.max(pick_ids[:, i : i + 1]) for i in range(n_picks)]
    copies = []
    for i in range(n_picks):
        at = pl.multiple_of(wanted[i] // SUBLANES * SUBLANES, SUBLANES)
        copies.append(
            pltpu.make_async_copy(
                pool.at[pl.ds(at, SUBLANES), :], tile.at[i], pick_sem.at[i]
            )
        )
        copies[-1].start()
    mine = pl.multiple_of(lax.rem(lax.axis_index("cand"), share) * count, count)
    moves, first = [], 0
    for k, piece in enumerate(pieces):
        source = queries.at[pl.ds(mine, count), first : first + piece.shape[1]]
        moves.append(pltpu.make_async_copy(source, piece, sems.at[k]))
        first += piece.shape[1]
    for move in moves:
        move.start()
    row = lax.broadcasted_iota(jnp.int32, (SUBLANES, LANES), 0)
    for i in range(n_picks):
        copies[i].wait()
        own = row == wanted[i] % SUBLANES
        for c in range(cut):
            some = tile[i, :, c * LANES : (c + 1) * LANES].astype(jnp.float32)
            lines[c : c + 1, :] = jnp.sum(
                jnp.where(own, some, 0.0), axis=0, keepdims=True
            )
        picks[i] = lines[...].astype(jnp.bfloat16)
    for move in moves:
        move.wait()


def chunks_of(depth):
    unit = LANES * math.gcd(depth // LANES, 4)
    first = depth * 5 // 8 // unit * unit
    return (first, depth - first)


def start(pool, pick_ids, queries, share):
    n_picks, depth = pick_ids.shape[0], pool.shape[1]
    widths = chunks_of(depth)
    return pl.pallas_call(
        functools.partial(start_kernel, share),
        in_specs=[VMEM, HBM, HBM],
        out_specs=[VMEM] * (1 + len(widths)),
        out_shape=[
            jax.ShapeDtypeStruct((n_picks, depth // LANES, LANES), pool.dtype),
        ]
        + [
            jax.ShapeDtypeStruct((queries.shape[0] // share, width), queries.dtype)
            for width in widths
        ],
        scratch_shapes=[
            pltpu.VMEM((n_picks, SUBLANES, depth), pool.dtype),
            pltpu.VMEM((depth // LANES, LANES), jnp.float32),
            pltpu.SemaphoreType.DMA((n_picks,)),
            pltpu.SemaphoreType.DMA((len(widths),)),
        ],
        compiler_params=PARAMS,
        cost_estimate=cost(0, 0, 0, 8 * pool.size),
        name="start",
    )(
        pick_ids.reshape(1, n_picks),
        pltpu.with_memory_space_constraint(pool, pltpu.HBM),
        pltpu.with_memory_space_constraint(queries, pltpu.HBM),
    )


def scores_kernel(first, start, width, pool, queries, *refs):
    pieces, out = refs[:-1], refs[-1]
    targets = [queries[:, start : start + width]] + [p[...] for p in pieces]
    targets = jnp.concatenate(targets, axis=0)
    step = math.gcd(out.shape[0], ROWS)
    for row in range(0, out.shape[0], step):
        out[row : row + step, :] = dot(
            pool[first + row : first + row + step, start : start + width], targets
        )


def scores(pool, queries, pieces, start, first, rows):
    width = pieces[0].shape[1] if pieces else queries.shape[1]
    count = queries.shape[0] + sum(p.shape[0] for p in pieces)
    return pl.pallas_call(
        functools.partial(scores_kernel, first, start, width),
        in_specs=[VMEM] * (2 + len(pieces)),
        out_specs=VMEM,
        out_shape=jax.ShapeDtypeStruct((rows, count), jnp.float32),
        compiler_params=PARAMS,
        cost_estimate=cost(rows, count, width),
        name="scores",
    )(pool, queries, *pieces)


def cover_kernel(groups, picks, *refs):
    best, wide = refs[-2:]
    refs = list(refs[:-2])
    blocks = [
        [[refs.pop(0) for _ in range(n_pieces)] for _ in range(n_chunks)]
        for n_chunks, n_pieces in groups
    ]
    n_picks, cut, _ = picks.shape
    lines = math.gcd(cut, 4)
    width = lines * LANES

    wide[...] = picks[...].astype(jnp.float32).reshape(n_picks * cut, LANES)
    total = None
    for j in range(cut // lines):
        rows = jnp.concatenate(
            [
                wide[pl.ds(j * lines + k, n_picks, stride=cut), :]
                for k in range(lines)
            ],
            axis=1,
        ).astype(jnp.bfloat16)
        some = []
        for block in blocks:
            at = j * width
            for pieces in block:
                held = pieces[0].shape[1]
                if 0 <= at < held:
                    some += [piece[:, at : at + width] for piece in pieces]
                at -= held
        term = dot(rows, jnp.concatenate(some, axis=0))
        total = term if total is None else total + term
    best[...] = jnp.max(total, axis=0, keepdims=True)


def cover_of(picks, blocks):
    groups = tuple((len(block), len(block[0])) for block in blocks)
    flat = [piece for block in blocks for pieces in block for piece in pieces]
    count = sum(piece.shape[0] for block in blocks for piece in block[0])
    n_picks, cut, _ = picks.shape
    return pl.pallas_call(
        functools.partial(cover_kernel, groups),
        in_specs=[VMEM] * (1 + len(flat)),
        out_specs=VMEM,
        out_shape=jax.ShapeDtypeStruct((1, count), jnp.float32),
        scratch_shapes=[pltpu.VMEM((n_picks * cut, LANES), jnp.float32)],
        compiler_params=PARAMS,
        cost_estimate=cost(2 * LANES, count, cut * LANES),
        name="cover",
    )(picks, *flat)


def gains_kernel(scale, n_bests, shape, ids, *refs):
    gains, cover = refs[-2:]
    refs = list(refs[:-2])
    best = refs.pop(0)[...]
    count = cover.shape[1]
    if n_bests == 2:
        theirs = refs.pop(0)[...]
        turned = [theirs[:, :count]]
        for at in range(count, best.shape[1], count):
            turned.append(pltpu.roll(theirs[:, at : at + count], count // 2, 1))
        best = jnp.maximum(best, jnp.concatenate(turned, axis=1))
    chunks = []
    for n_arrays in shape:
        lines = []
        for _ in range(n_arrays):
            ref = refs.pop(0)
            lines += [(ref, row) for row in range(0, ref.shape[0], LANES)]
        chunks.append(lines)
    cover[...] = best[:, :count] * scale

    row = lax.broadcasted_iota(jnp.int32, (LANES, LANES), 0)
    lane = lax.broadcasted_iota(jnp.int32, (LANES, LANES), 1)
    diagonal = row == lane
    wanted = ids[...]
    block_wanted, lane_wanted = wanted // LANES, wanted % LANES
    found = jnp.zeros(wanted.shape, jnp.float32)
    for block, every in enumerate(zip(*chunks)):
        above, highest = None, None
        for at in range(0, best.shape[1], LANES):
            some = slice(at, at + LANES)
            s = None
            for ref, first in every:
                term = ref[first : first + LANES, some]
                s = term if s is None else s + term
            over = jnp.maximum(s - best[:, some], 0.0)
            above = over if above is None else above + over
            highest = s if highest is None else jnp.maximum(highest, s)
        gain = jnp.sum(above, axis=1, keepdims=True) + 1.0 * jnp.max(
            highest, axis=1, keepdims=True
        )
        line = jnp.sum(jnp.where(diagonal, gain, 0.0), axis=0, keepdims=True)
        table = jnp.broadcast_to(line, wanted.shape)
        here = jnp.take_along_axis(table, lane_wanted, axis=1, mode="promise_in_bounds")
        found = jnp.where(block_wanted == block, here, found)
    gains[...] = found * scale


def gains_of(bests, ids, parts, count, scale):
    flat = bests + [p for part in parts for p in part]
    return pl.pallas_call(
        functools.partial(gains_kernel, scale, len(bests), tuple(map(len, parts))),
        in_specs=[VMEM] * (1 + len(flat)),
        out_shape=(
            jax.ShapeDtypeStruct(ids.shape, jnp.float32),
            jax.ShapeDtypeStruct((1, count), jnp.float32),
        ),
        compiler_params=PARAMS,
        name="gains",
    )(ids, *flat)


def strides(size):
    if size & (size - 1):
        return None
    return [size >> (k + 1) for k in range(size.bit_length() - 1)]


def gather_over(x, axis, size, least=1):
    if strides(size) is None:
        rest = [
            lax.ppermute(x, axis, [(i, (i + s) % size) for i in range(size)])
            for s in range(1, size)
        ]
        return jnp.concatenate([x] + rest, axis=0)
    for bit in strides(size):
        if bit >= least:
            got = lax.ppermute(x, axis, [(i, i ^ bit) for i in range(size)])
            x = jnp.concatenate([x, got], axis=0)
    return x


def on_device(sizes, pool, cand_ids, pick_ids, queries):
    n_cand, n_query = sizes
    rows, depth = pool.shape
    scale = 1.0 / math.sqrt(depth)
    mates = [(i, i ^ 1) for i in range(n_cand)]

    share = 2 if n_cand % 2 == 0 else 1
    picks, *sent = start(pool, pick_ids, queries, share)
    held = queries

    swapped = bool(strides(n_cand))
    picks = gather_over(picks, "query", n_query)
    picks = gather_over(picks, "cand", n_cand, 2 if swapped else 1)

    blocks = [[[held]]]
    for shift in range(1, n_query):
        block = []
        for piece in sent:
            got = lax.ppermute(
                piece,
                "query",
                [(i, (i + shift) % n_query) for i in range(n_query)],
            )
            both = [got]
            if share == 2:
                both.append(lax.ppermute(got, "cand", mates))
            block.append(both)
        blocks.append(block)

    parts, start_at = [], 0
    for chunk, piece in enumerate(sent):
        pieces = [p for block in blocks[1:] for p in block[chunk]]
        part, first = [], 0
        for k in range(PARTS[chunk]):
            some = rows * (k + 1) // PARTS[chunk] // LANES * LANES - first
            part.append(scores(pool, held, pieces, start_at, first, some))
            first += some
        parts.append(part)
        start_at += piece.shape[1]

    bests = [cover_of(picks, blocks)]
    if swapped:
        bests.append(lax.ppermute(bests[0], "cand", mates))
    gains, cover = gains_of(
        bests, cand_ids.reshape(-1, LANES), parts, queries.shape[0], scale
    )
    return gains.reshape(cand_ids.shape), cover.reshape(queries.shape[:1])


def solution(mesh):
    sizes = (mesh.shape["cand"], mesh.shape["query"])
    in_specs = (
        P(("cand", "query"), None),
        P(("cand", "query")),
        P(("cand", "query")),
        P("query", None),
    )
    out_specs = (P(("cand", "query")), P("query"))

    def body(*args):
        return on_device(sizes, *args)

    return jax.shard_map(
        body, mesh=mesh, in_specs=in_specs, out_specs=out_specs, check_vma=False
    )
```

```python
import functools
import math

import jax
import jax.numpy as jnp
from jax import lax
from jax.experimental import pallas as pl
from jax.experimental.pallas import tpu as pltpu
from jax.sharding import PartitionSpec as P

LANES = 128
SUBLANES = 8
PARTS = 2
ROWS = 640
NT = (((1,), (1,)), ((), ()))
VMEM = pl.BlockSpec(memory_space=pltpu.VMEM)
HBM = pl.BlockSpec(memory_space=pltpu.HBM)
PARAMS = pltpu.CompilerParams(vmem_limit_bytes=12 * 2**20)


def dot(rows, targets):
    return lax.dot_general(rows, targets, NT, preferred_element_type=jnp.float32)


def cost(rows, count, width, read=0):
    return pl.CostEstimate(
        flops=2 * rows * max(count, 256) * width,
        bytes_accessed=rows * width * 2 + read,
        transcendentals=0,
    )


def start_kernel(share, pick_ids, pool, queries, *refs):
    picks, *pieces, tile, lines, pick_sem, sems = refs
    n_picks, cut, _ = picks.shape
    count = pieces[0].shape[0]
    wanted = [pick_ids[i] for i in range(n_picks)]
    copies = []
    for i in range(n_picks):
        at = pl.multiple_of(wanted[i] // SUBLANES * SUBLANES, SUBLANES)
        copies.append(
            pltpu.make_async_copy(
                pool.at[pl.ds(at, SUBLANES), :], tile.at[i], pick_sem.at[i]
            )
        )
        copies[-1].start()
    mine = pl.multiple_of(lax.rem(lax.axis_index("cand"), share) * count, count)
    moves, first = [], 0
    for k, piece in enumerate(pieces):
        source = queries.at[pl.ds(mine, count), first : first + piece.shape[1]]
        moves.append(pltpu.make_async_copy(source, piece, sems.at[k]))
        first += piece.shape[1]
    for move in moves:
        move.start()
    row = lax.broadcasted_iota(jnp.int32, (SUBLANES, LANES), 0)
    for i in range(n_picks):
        copies[i].wait()
        own = row == wanted[i] % SUBLANES
        for c in range(cut):
            some = tile[i, :, c * LANES : (c + 1) * LANES].astype(jnp.float32)
            lines[c : c + 1, :] = jnp.sum(
                jnp.where(own, some, 0.0), axis=0, keepdims=True
            )
        picks[i] = lines[...].astype(jnp.bfloat16)
    for move in moves:
        move.wait()


def chunks_of(depth):
    unit = LANES * math.gcd(depth // LANES, 4)
    first = depth * 5 // 8 // unit * unit
    return (first, depth - first)


def start(pool, pick_ids, queries, share):
    n_picks, depth = pick_ids.shape[0], pool.shape[1]
    widths = chunks_of(depth)
    return pl.pallas_call(
        functools.partial(start_kernel, share),
        in_specs=[pl.BlockSpec(memory_space=pltpu.SMEM), HBM, HBM],
        out_specs=[VMEM] * (1 + len(widths)),
        out_shape=[
            jax.ShapeDtypeStruct((n_picks, depth // LANES, LANES), pool.dtype),
        ]
        + [
            jax.ShapeDtypeStruct((queries.shape[0] // share, width), queries.dtype)
            for width in widths
        ],
        scratch_shapes=[
            pltpu.VMEM((n_picks, SUBLANES, depth), pool.dtype),
            pltpu.VMEM((depth // LANES, LANES), jnp.float32),
            pltpu.SemaphoreType.DMA((n_picks,)),
            pltpu.SemaphoreType.DMA((len(widths),)),
        ],
        compiler_params=PARAMS,
        cost_estimate=cost(0, 0, 0, 8 * pool.size),
        name="start",
    )(
        pick_ids,
        pltpu.with_memory_space_constraint(pool, pltpu.HBM),
        pltpu.with_memory_space_constraint(queries, pltpu.HBM),
    )


def targets_of(queries, pieces, start):
    width = pieces[0].shape[1] if pieces else queries.shape[1]
    return jnp.concatenate(
        [queries[:, start : start + width]] + [p[...] for p in pieces], axis=0
    )


def scores_kernel(first, start, width, pool, queries, *refs):
    pieces, out = refs[:-1], refs[-1]
    targets = targets_of(queries, pieces, start)
    step = math.gcd(out.shape[0], ROWS)
    for row in range(0, out.shape[0], step):
        out[row : row + step, :] = dot(
            pool[first + row : first + row + step, start : start + width], targets
        )


def scores(pool, queries, pieces, start, first, rows):
    width = pieces[0].shape[1] if pieces else queries.shape[1]
    count = queries.shape[0] + sum(p.shape[0] for p in pieces)
    return pl.pallas_call(
        functools.partial(scores_kernel, first, start, width),
        in_specs=[VMEM] * (2 + len(pieces)),
        out_specs=VMEM,
        out_shape=jax.ShapeDtypeStruct((rows, count), jnp.float32),
        compiler_params=PARAMS,
        cost_estimate=cost(rows, count, width),
        name="scores",
    )(pool, queries, *pieces)


def diagonal():
    row = lax.broadcasted_iota(jnp.int32, (LANES, LANES), 0)
    return row == lax.broadcasted_iota(jnp.int32, (LANES, LANES), 1)


def in_line(column, keep):
    return jnp.sum(jnp.where(keep, column, 0.0), axis=0, keepdims=True)


def totals_kernel(start, width, n_before, pool, queries, *refs):
    before, pieces = refs[:n_before], refs[n_before:-2]
    out, top = refs[-2:]
    targets = targets_of(queries, pieces, start)
    keep = diagonal()
    first = 0
    for ref in before:
        step = math.gcd(ref.shape[0], ROWS)
        for row in range(0, ref.shape[0], step):
            at = first + row
            last = dot(pool[at : at + step, start : start + width], targets)
            for k in range(0, step, LANES):
                s = ref[row + k : row + k + LANES, :] + last[k : k + LANES, :]
                out[at + k : at + k + LANES, :] = s
                highest = jnp.max(s, axis=1, keepdims=True)
                block = (at + k) // LANES
                top[block : block + 1, :] = in_line(highest, keep)
        first += ref.shape[0]


def totals(pool, queries, before, pieces, start):
    width = pieces[0].shape[1] if pieces else queries.shape[1]
    rows, count = sum(b.shape[0] for b in before), before[0].shape[1]
    return pl.pallas_call(
        functools.partial(totals_kernel, start, width, len(before)),
        in_specs=[VMEM] * (2 + len(before) + len(pieces)),
        out_specs=[VMEM, VMEM],
        out_shape=[
            jax.ShapeDtypeStruct((rows, count), jnp.float32),
            jax.ShapeDtypeStruct((rows // LANES, LANES), jnp.float32),
        ],
        compiler_params=PARAMS,
        cost_estimate=cost(rows, count, width),
        name="totals",
    )(pool, queries, *before, *pieces)


def cover_kernel(groups, picks, *refs):
    best, wide = refs[-2:]
    refs = list(refs[:-2])
    blocks = [
        [[refs.pop(0) for _ in range(n_pieces)] for _ in range(n_chunks)]
        for n_chunks, n_pieces in groups
    ]
    n_picks, cut, _ = picks.shape
    lines = math.gcd(cut, 4)
    width = lines * LANES

    wide[...] = picks[...].astype(jnp.float32).reshape(n_picks * cut, LANES)
    total = None
    for j in range(cut // lines):
        rows = jnp.concatenate(
            [
                wide[pl.ds(j * lines + k, n_picks, stride=cut), :]
                for k in range(lines)
            ],
            axis=1,
        ).astype(jnp.bfloat16)
        some = []
        for block in blocks:
            at = j * width
            for pieces in block:
                held = pieces[0].shape[1]
                if 0 <= at < held:
                    some += [piece[:, at : at + width] for piece in pieces]
                at -= held
        term = dot(rows, jnp.concatenate(some, axis=0))
        total = term if total is None else total + term
    best[...] = jnp.max(total, axis=0, keepdims=True)


def cover_of(picks, blocks):
    groups = tuple((len(block), len(block[0])) for block in blocks)
    flat = [piece for block in blocks for pieces in block for piece in pieces]
    count = sum(piece.shape[0] for block in blocks for piece in block[0])
    n_picks, cut, _ = picks.shape
    return pl.pallas_call(
        functools.partial(cover_kernel, groups),
        in_specs=[VMEM] * (1 + len(flat)),
        out_specs=VMEM,
        out_shape=jax.ShapeDtypeStruct((1, count), jnp.float32),
        scratch_shapes=[pltpu.VMEM((n_picks * cut, LANES), jnp.float32)],
        compiler_params=PARAMS,
        cost_estimate=cost(2 * LANES, count, cut * LANES),
        name="cover",
    )(picks, *flat)


def gains_kernel(scale, ids, total, top, *refs):
    bests, (gains, cover) = refs[:-2], refs[-2:]
    best = bests[0][...]
    count = cover.shape[1]
    if len(bests) == 2:
        theirs = bests[1][...]
        turned = [theirs[:, :count]]
        for at in range(count, best.shape[1], count):
            turned.append(pltpu.roll(theirs[:, at : at + count], count // 2, 1))
        best = jnp.maximum(best, jnp.concatenate(turned, axis=1))
    cover[...] = best[:, :count] * scale

    keep = diagonal()
    wanted = ids[...]
    block_wanted, lane_wanted = wanted // LANES, wanted % LANES
    found = jnp.zeros(wanted.shape, jnp.float32)
    for block in range(top.shape[0]):
        s = total[block * LANES : (block + 1) * LANES, :]
        above = jnp.sum(jnp.maximum(s - best, 0.0), axis=1, keepdims=True)
        line = in_line(above, keep) + 1.0 * top[block : block + 1, :]
        table = jnp.broadcast_to(line, wanted.shape)
        here = jnp.take_along_axis(table, lane_wanted, axis=1, mode="promise_in_bounds")
        found = jnp.where(block_wanted == block, here, found)
    gains[...] = found * scale


def gains_of(bests, ids, total, top, count, scale):
    return pl.pallas_call(
        functools.partial(gains_kernel, scale),
        in_specs=[VMEM] * (3 + len(bests)),
        out_shape=(
            jax.ShapeDtypeStruct(ids.shape, jnp.float32),
            jax.ShapeDtypeStruct((1, count), jnp.float32),
        ),
        compiler_params=PARAMS,
        name="gains",
    )(ids, total, top, *bests)


def is_power(size):
    return size & (size - 1) == 0


def stages(n_cand, n_query):
    n = n_cand * n_query
    bits = [1 << k for k in range(n.bit_length() - 1) if 1 << k != n_query]
    rounds = [[bit] for bit in bits]
    if len(bits) > 1:
        low, high = bits[-2:]
        rounds[-2:] = [[low | high, high, low]]
    return rounds


def gather_over(x, n_cand, n_query, swapped):
    both, n = ("cand", "query"), n_cand * n_query
    if not swapped:
        rest = [
            lax.ppermute(x, both, [(i, (i + s) % n) for i in range(n)])
            for s in range(1, n)
        ]
        return jnp.concatenate([x] + rest, axis=0)
    for masks in stages(n_cand, n_query):
        got = []
        for mask in masks:
            got.append(lax.ppermute(x, both, [(i, i ^ mask) for i in range(n)]))
        x = jnp.concatenate([x] + got, axis=0)
    return x


def on_device(sizes, pool, cand_ids, pick_ids, queries):
    n_cand, n_query = sizes
    rows, depth = pool.shape
    scale = 1.0 / math.sqrt(depth)
    mates = [(i, i ^ 1) for i in range(n_cand)]

    share = 2 if n_cand % 2 == 0 else 1
    picks, *sent = start(pool, pick_ids, queries, share)
    held = queries

    swapped = n_cand > 1 and is_power(n_cand) and is_power(n_query)
    picks = gather_over(picks, n_cand, n_query, swapped)

    blocks = [[[held]]]
    for shift in range(1, n_query):
        block = []
        for piece in sent:
            got = lax.ppermute(
                piece,
                "query",
                [(i, (i + shift) % n_query) for i in range(n_query)],
            )
            both = [got]
            if share == 2:
                both.append(lax.ppermute(got, "cand", mates))
            block.append(both)
        blocks.append(block)

    pieces = [p for block in blocks[1:] for p in block[0]]
    before, first = [], 0
    for k in range(PARTS):
        some = rows * (k + 1) // PARTS // LANES * LANES - first
        before.append(scores(pool, held, pieces, 0, first, some))
        first += some
    pieces = [p for block in blocks[1:] for p in block[1]]
    total, top = totals(pool, held, before, pieces, sent[0].shape[1])

    bests = [cover_of(picks, blocks)]
    if swapped:
        bests.append(lax.ppermute(bests[0], "cand", mates))
    gains, cover = gains_of(
        bests, cand_ids.reshape(-1, LANES), total, top, queries.shape[0], scale
    )
    return gains.reshape(cand_ids.shape), cover.reshape(queries.shape[:1])


def solution(mesh):
    sizes = (mesh.shape["cand"], mesh.shape["query"])
    in_specs = (
        P(("cand", "query"), None),
        P(("cand", "query")),
        P(("cand", "query")),
        P("query", None),
    )
    out_specs = (P(("cand", "query")), P("query"))

    def body(*args):
        return on_device(sizes, *args)

    return jax.shard_map(
        body, mesh=mesh, in_specs=in_specs, out_specs=out_specs, check_vma=False
    )
```

```python
import functools
import math

import jax
import jax.numpy as jnp
from jax import lax
from jax.experimental import pallas as pl
from jax.experimental.pallas import tpu as pltpu
from jax.sharding import PartitionSpec as P

LANES = 128
SUBLANES = 8
PARTS = 2
ROWS = 640
NT = (((1,), (1,)), ((), ()))
VMEM = pl.BlockSpec(memory_space=pltpu.VMEM)
HBM = pl.BlockSpec(memory_space=pltpu.HBM)
PARAMS = pltpu.CompilerParams(vmem_limit_bytes=12 * 2**20)


def dot(rows, targets):
    return lax.dot_general(rows, targets, NT, preferred_element_type=jnp.float32)


def cost(rows, count, width, read=0):
    return pl.CostEstimate(
        flops=2 * rows * max(count, 256) * width,
        bytes_accessed=rows * width * 2 + read,
        transcendentals=0,
    )


def start_kernel(share, pick_ids, pool, queries, *refs):
    picks, *pieces, tile, lines, pick_sem, sems = refs
    n_picks, cut, _ = picks.shape
    count = pieces[0].shape[0]
    wanted = [pick_ids[i] for i in range(n_picks)]
    copies = []
    for i in range(n_picks):
        at = pl.multiple_of(wanted[i] // SUBLANES * SUBLANES, SUBLANES)
        copies.append(
            pltpu.make_async_copy(
                pool.at[pl.ds(at, SUBLANES), :], tile.at[i], pick_sem.at[i]
            )
        )
        copies[-1].start()
    mine = pl.multiple_of(lax.rem(lax.axis_index("cand"), share) * count, count)
    moves, first = [], 0
    for k, piece in enumerate(pieces):
        source = queries.at[pl.ds(mine, count), first : first + piece.shape[1]]
        moves.append(pltpu.make_async_copy(source, piece, sems.at[k]))
        first += piece.shape[1]
    for move in moves:
        move.start()
    row = lax.broadcasted_iota(jnp.int32, (SUBLANES, LANES), 0)
    for i in range(n_picks):
        copies[i].wait()
        own = row == wanted[i] % SUBLANES
        for c in range(cut):
            some = tile[i, :, c * LANES : (c + 1) * LANES].astype(jnp.float32)
            lines[c : c + 1, :] = jnp.sum(
                jnp.where(own, some, 0.0), axis=0, keepdims=True
            )
        picks[i] = lines[...].astype(jnp.bfloat16)
    for move in moves:
        move.wait()


def chunks_of(depth):
    unit = LANES * math.gcd(depth // LANES, 4)
    first = depth * 5 // 8 // unit * unit
    return (first, depth - first)


def start(pool, pick_ids, queries, share):
    n_picks, depth = pick_ids.shape[0], pool.shape[1]
    widths = chunks_of(depth)
    return pl.pallas_call(
        functools.partial(start_kernel, share),
        in_specs=[pl.BlockSpec(memory_space=pltpu.SMEM), HBM, HBM],
        out_specs=[VMEM] * (1 + len(widths)),
        out_shape=[
            jax.ShapeDtypeStruct((n_picks, depth // LANES, LANES), pool.dtype),
        ]
        + [
            jax.ShapeDtypeStruct((queries.shape[0] // share, width), queries.dtype)
            for width in widths
        ],
        scratch_shapes=[
            pltpu.VMEM((n_picks, SUBLANES, depth), pool.dtype),
            pltpu.VMEM((depth // LANES, LANES), jnp.float32),
            pltpu.SemaphoreType.DMA((n_picks,)),
            pltpu.SemaphoreType.DMA((len(widths),)),
        ],
        compiler_params=PARAMS,
        cost_estimate=cost(0, 0, 0, 8 * pool.size),
        name="start",
    )(
        pick_ids,
        pltpu.with_memory_space_constraint(pool, pltpu.HBM),
        pltpu.with_memory_space_constraint(queries, pltpu.HBM),
    )


def targets_of(queries, pieces, start):
    width = pieces[0].shape[1] if pieces else queries.shape[1]
    return jnp.concatenate(
        [queries[:, start : start + width]] + [p[...] for p in pieces], axis=0
    )


def scores_kernel(first, start, width, pool, queries, *refs):
    pieces, out = refs[:-1], refs[-1]
    targets = targets_of(queries, pieces, start)
    step = math.gcd(out.shape[0], ROWS)
    for row in range(0, out.shape[0], step):
        out[row : row + step, :] = dot(
            pool[first + row : first + row + step, start : start + width], targets
        )


def scores(pool, queries, pieces, start, first, rows):
    width = pieces[0].shape[1] if pieces else queries.shape[1]
    count = queries.shape[0] + sum(p.shape[0] for p in pieces)
    return pl.pallas_call(
        functools.partial(scores_kernel, first, start, width),
        in_specs=[VMEM] * (2 + len(pieces)),
        out_specs=VMEM,
        out_shape=jax.ShapeDtypeStruct((rows, count), jnp.float32),
        compiler_params=PARAMS,
        cost_estimate=cost(rows, count, width),
        name="scores",
    )(pool, queries, *pieces)


def diagonal():
    row = lax.broadcasted_iota(jnp.int32, (LANES, LANES), 0)
    return row == lax.broadcasted_iota(jnp.int32, (LANES, LANES), 1)


def in_line(column, keep):
    return jnp.sum(jnp.where(keep, column, 0.0), axis=0, keepdims=True)


def totals_kernel(start, width, n_before, pool, queries, *refs):
    before, pieces = refs[:n_before], refs[n_before:-2]
    out, top = refs[-2:]
    targets = targets_of(queries, pieces, start)
    keep = diagonal()
    first = 0
    for ref in before:
        step = math.gcd(ref.shape[0], ROWS)
        for row in range(0, ref.shape[0], step):
            at = first + row
            last = dot(pool[at : at + step, start : start + width], targets)
            for k in range(0, step, LANES):
                s = ref[row + k : row + k + LANES, :] + last[k : k + LANES, :]
                out[at + k : at + k + LANES, :] = s
                highest = jnp.max(s, axis=1, keepdims=True)
                block = (at + k) // LANES
                top[block : block + 1, :] = in_line(highest, keep)
        first += ref.shape[0]


def totals(pool, queries, before, pieces, start):
    width = pieces[0].shape[1] if pieces else queries.shape[1]
    rows, count = sum(b.shape[0] for b in before), before[0].shape[1]
    return pl.pallas_call(
        functools.partial(totals_kernel, start, width, len(before)),
        in_specs=[VMEM] * (2 + len(before) + len(pieces)),
        out_specs=[VMEM, VMEM],
        out_shape=[
            jax.ShapeDtypeStruct((rows, count), jnp.float32),
            jax.ShapeDtypeStruct((rows // LANES, LANES), jnp.float32),
        ],
        compiler_params=PARAMS,
        cost_estimate=cost(rows, count, width),
        name="totals",
    )(pool, queries, *before, *pieces)


def cover_kernel(groups, picks, *refs):
    best, sent, wide = refs[-3:]
    refs = list(refs[:-3])
    blocks = [
        [[refs.pop(0) for _ in range(n_pieces)] for _ in range(n_chunks)]
        for n_chunks, n_pieces in groups
    ]
    n_picks, cut, _ = picks.shape
    lines = math.gcd(cut, 4)
    width = lines * LANES

    wide[...] = picks[...].astype(jnp.float32).reshape(n_picks * cut, LANES)
    total = None
    for j in range(cut // lines):
        rows = jnp.concatenate(
            [
                wide[pl.ds(j * lines + k, n_picks, stride=cut), :]
                for k in range(lines)
            ],
            axis=1,
        ).astype(jnp.bfloat16)
        some = []
        for block in blocks:
            at = j * width
            for pieces in block:
                held = pieces[0].shape[1]
                if 0 <= at < held:
                    some += [piece[:, at : at + width] for piece in pieces]
                at -= held
        term = dot(rows, jnp.concatenate(some, axis=0))
        total = term if total is None else total + term
    found = jnp.max(total, axis=0, keepdims=True)
    best[...] = found
    count = blocks[0][0][0].shape[0]
    turned = [found[:, :count]]
    for at in range(count, found.shape[1], count):
        turned.append(pltpu.roll(found[:, at : at + count], count // 2, 1))
    sent[...] = jnp.concatenate(turned, axis=1)


def cover_of(picks, blocks):
    groups = tuple((len(block), len(block[0])) for block in blocks)
    flat = [piece for block in blocks for pieces in block for piece in pieces]
    count = sum(piece.shape[0] for block in blocks for piece in block[0])
    n_picks, cut, _ = picks.shape
    return pl.pallas_call(
        functools.partial(cover_kernel, groups),
        in_specs=[VMEM] * (1 + len(flat)),
        out_specs=[VMEM, VMEM],
        out_shape=[jax.ShapeDtypeStruct((1, count), jnp.float32)] * 2,
        scratch_shapes=[pltpu.VMEM((n_picks * cut, LANES), jnp.float32)],
        compiler_params=PARAMS,
        cost_estimate=cost(2 * LANES, count, cut * LANES),
        name="cover",
    )(picks, *flat)


def gains_kernel(scale, ids, total, top, *refs):
    bests, (gains, cover) = refs[:-2], refs[-2:]
    best = bests[0][...]
    count = cover.shape[1]
    if len(bests) == 2:
        best = jnp.maximum(best, bests[1][...])
    cover[...] = best[:, :count] * scale

    keep = diagonal()
    wanted = ids[...]
    block_wanted, lane_wanted = wanted // LANES, wanted % LANES
    found = jnp.zeros(wanted.shape, jnp.float32)
    for block in range(top.shape[0]):
        s = total[block * LANES : (block + 1) * LANES, :]
        above = jnp.sum(jnp.maximum(s - best, 0.0), axis=1, keepdims=True)
        line = in_line(above, keep) + 1.0 * top[block : block + 1, :]
        table = jnp.broadcast_to(line, wanted.shape)
        here = jnp.take_along_axis(table, lane_wanted, axis=1, mode="promise_in_bounds")
        found = jnp.where(block_wanted == block, here, found)
    gains[...] = found * scale


def gains_of(bests, ids, total, top, count, scale):
    return pl.pallas_call(
        functools.partial(gains_kernel, scale),
        in_specs=[VMEM] * (3 + len(bests)),
        out_shape=(
            jax.ShapeDtypeStruct(ids.shape, jnp.float32),
            jax.ShapeDtypeStruct((1, count), jnp.float32),
        ),
        compiler_params=PARAMS,
        name="gains",
    )(ids, total, top, *bests)


def is_power(size):
    return size & (size - 1) == 0


def stages(n_cand, n_query):
    n = n_cand * n_query
    bits = [1 << k for k in range(n.bit_length() - 1) if 1 << k != n_query]
    rounds = [[bit] for bit in bits]
    if len(bits) > 1:
        low, high = bits[-2:]
        rounds[-2:] = [[low | high, low, high]]
    return rounds


def gather_over(x, n_cand, n_query, swapped):
    both, n = ("cand", "query"), n_cand * n_query
    if not swapped:
        rest = [
            lax.ppermute(x, both, [(i, (i + s) % n) for i in range(n)])
            for s in range(1, n)
        ]
        return jnp.concatenate([x] + rest, axis=0)
    for masks in stages(n_cand, n_query):
        got = []
        for mask in masks:
            got.append(lax.ppermute(x, both, [(i, i ^ mask) for i in range(n)]))
        x = jnp.concatenate([x] + got, axis=0)
    return x


def on_device(sizes, pool, cand_ids, pick_ids, queries):
    n_cand, n_query = sizes
    rows, depth = pool.shape
    scale = 1.0 / math.sqrt(depth)
    mates = [(i, i ^ 1) for i in range(n_cand)]

    share = 2 if n_cand % 2 == 0 else 1
    picks, *sent = start(pool, pick_ids, queries, share)
    held = queries

    swapped = n_cand > 1 and is_power(n_cand) and is_power(n_query)
    picks = gather_over(picks, n_cand, n_query, swapped)

    blocks = [[[held]]]
    for shift in range(1, n_query):
        block = []
        for piece in sent:
            got = lax.ppermute(
                piece,
                "query",
                [(i, (i + shift) % n_query) for i in range(n_query)],
            )
            both = [got]
            if share == 2:
                both.append(lax.ppermute(got, "cand", mates))
            block.append(both)
        blocks.append(block)

    pieces = [p for block in blocks[1:] for p in block[0]]
    before, first = [], 0
    for k in range(PARTS):
        some = rows * (k + 1) // PARTS // LANES * LANES - first
        before.append(scores(pool, held, pieces, 0, first, some))
        first += some
    pieces = [p for block in blocks[1:] for p in block[1]]
    total, top = totals(pool, held, before, pieces, sent[0].shape[1])

    best, turned = cover_of(picks, blocks)
    bests = [best]
    if swapped:
        bests.append(lax.ppermute(turned, "cand", mates))
    gains, cover = gains_of(
        bests, cand_ids.reshape(-1, LANES), total, top, queries.shape[0], scale
    )
    return gains.reshape(cand_ids.shape), cover.reshape(queries.shape[:1])


def solution(mesh):
    sizes = (mesh.shape["cand"], mesh.shape["query"])
    in_specs = (
        P(("cand", "query"), None),
        P(("cand", "query")),
        P(("cand", "query")),
        P("query", None),
    )
    out_specs = (P(("cand", "query")), P("query"))

    def body(*args):
        return on_device(sizes, *args)

    return jax.shard_map(
        body, mesh=mesh, in_specs=in_specs, out_specs=out_specs, check_vma=False
    )
```
